128 devices in a mesh: row: 8 (over x, y_lo), col: 8 (over z, y_hi), depth: 2 (over core).
Axes of the slice: x: 4, y: 4 (y_hi: 2, y_lo: 2; y = y_hi * 2 + y_lo), z: 4, core: 2. Of those that a mesh axis runs over, the one named last changes fastest.
Arguments:
- amplitudes: bfloat16 [20480, 20480], P('row', 'col'), may hold values from -0.109375 to 0.109375
- coulomb_vertex: bfloat16 [256, 20480], P('depth', ('row', 'col')), may hold values from -1.5 to 1.5
Outputs:
- cycle_residual: bfloat16 [20480, 20480], P('row', ('col', 'depth'))
- structure_factor: float32 [256], P('depth')
The draws below stay inside these ranges and needn't reach their ends.
All inputs are finite; a program needn't handle non-finite values.
Results may differ from the reference program's by a relative error of at most 0.0057.
Values may be sent and summed in bfloat16 or wider, within the bound.
No kernel may reach another device: no remote copies, remote signals or barrier semaphores. Data moves between devices by JAX's collectives and lax.ppermute only.
A program may use at most 128 MiB of HBM per device.

```python
import jax
import jax.numpy as jnp
from jax import lax

VIR = 1024
NG = 256
OCC = 20
PAIRS = 20480


def block_levels(rng, shape, pieces, smallest, high):
    loudness, own = 1.0, jax.random.fold_in(rng, 6)
    for axis_at, blocks in pieces:
        heights = jnp.exp(jax.random.uniform(jax.random.fold_in(own, axis_at), (blocks,), jnp.float32, smallest / len(pieces), high / len(pieces)))
        loudness = loudness * jnp.repeat(heights, shape[axis_at] // blocks).reshape([-1 if axis == axis_at else 1 for axis in range(len(shape))])
    return loudness


def noise(key, extent, deviation, limit, pieces=(), kind=jnp.bfloat16):
    values = jax.random.normal(key, extent, jnp.float32) * deviation
    if len(pieces) > 0:
        values = block_levels(key, extent, pieces, -0.22, 0.18) * values
    return jnp.clip(values, min=-limit, max=limit).astype(kind)


def setup_inputs(seed: int = 0) -> dict:
    key_of = jax.random.split(jax.random.key(seed), 3)
    amplitudes = noise(key_of[0], (PAIRS, PAIRS), (PAIRS ** -0.5), 0.109375, ((0, 8), (1, 8)))
    coulomb_vertex = noise(key_of[1], (NG, PAIRS), 0.25, 1.5, ((0, 2), (1, 64)))
    return {"amplitudes": amplitudes, "coulomb_vertex": coulomb_vertex}


def reference(amplitudes, coulomb_vertex):
    dressing = jnp.dot(coulomb_vertex, amplitudes, preferred_element_type=jnp.float32)
    structure_factor = jnp.sum(coulomb_vertex.astype(jnp.float32) * dressing, axis=1)
    dressed = (coulomb_vertex.astype(jnp.float32) + dressing).astype(jnp.bfloat16)
    blocks = jnp.moveaxis(dressed.reshape(NG, OCC, VIR), 1, 0)

    def one_block(piece):
        part = lax.dot_general(piece, dressed, (((0,), (0,)), ((), ())), preferred_element_type=jnp.float32)
        return part.astype(jnp.bfloat16)

    cycle_residual = lax.map(one_block, blocks).reshape(PAIRS, PAIRS)
    return cycle_residual, structure_factor
```

```python
import jax
import jax.numpy as jnp
from jax import lax
from jax.sharding import PartitionSpec as P

F32 = jnp.float32
BF16 = jnp.bfloat16


def split_three(x):
    parts = []
    for _ in range(3):
        head = lax.reduce_precision(x, 8, 7)
        parts.append(head.astype(BF16))
        x = x - head
    return jnp.stack(parts)


def gather_blocks(block, axis):
    copies = jnp.broadcast_to(block[None], (lax.axis_size(axis),) + block.shape)
    return lax.all_to_all(copies, axis, 0, 0)


def body(amplitudes, coulomb_vertex):
    rows = lax.axis_size("row")
    cols = lax.axis_size("col")
    fields, width = coulomb_vertex.shape
    depth_index = lax.axis_index("depth")
    across = [(r * cols + c, c * rows + r) for r in range(rows) for c in range(cols)]

    shard = coulomb_vertex.T
    shard_across = lax.ppermute(shard, ("row", "col"), across)
    vertex_rows = gather_blocks(shard, "col").reshape(-1, fields)
    partial = lax.dot_general(
        vertex_rows, amplitudes, (((0,), (0,)), ((), ())), preferred_element_type=F32
    )
    partial = partial.T.astype(BF16).reshape(rows, width, fields)
    partial = lax.all_to_all(partial, "row", 0, 0)
    dressing = jnp.sum(partial.astype(F32), axis=0)
    shard_across = shard_across.astype(F32)
    factor = jnp.sum(shard_across * dressing, axis=0)
    dressed = (shard_across + dressing).astype(BF16)

    pad = jnp.zeros((13, fields), BF16)
    block = jnp.concatenate([dressed, split_three(factor), pad])
    along = gather_blocks(block, "col")
    factor = jnp.sum(along[:, width : width + 3].astype(F32), axis=(0, 1))
    tail = jnp.concatenate([dressed, split_three(factor), pad])
    chunks = jnp.concatenate(
        [along[:, :width], jnp.broadcast_to(tail[None], (rows,) + tail.shape)], axis=1
    )
    arrived = lax.all_to_all(chunks, "row", 0, 0)
    structure_factor = jnp.sum(arrived[:, 2 * width : 2 * width + 3].astype(F32), axis=(0, 1))
    row_block = arrived[:, :width].reshape(-1, fields)
    col_block = arrived[:, width : 2 * width].reshape(-1, fields)

    half = col_block.shape[0] // 2
    swap = [(0, 1), (1, 0)]
    cols_mine = lax.dynamic_slice_in_dim(col_block, depth_index * half, half, 0)
    cols_send = lax.dynamic_slice_in_dim(col_block, (1 - depth_index) * half, half, 0)
    cols_other = lax.ppermute(cols_send, "depth", swap)
    rows_other = lax.ppermute(row_block, "depth", swap)
    left = jnp.concatenate([row_block, rows_other], axis=1)
    right = jnp.concatenate([cols_mine, cols_other], axis=1)
    product = lax.dot_general(
        left, right, (((1,), (1,)), ((), ())), preferred_element_type=F32
    )
    return (product.astype(BF16), structure_factor)


def solution(mesh):
    return jax.shard_map(
        body,
        mesh=mesh,
        in_specs=(P("row", "col"), P("depth", ("row", "col"))),
        out_specs=(P("row", ("col", "depth")), P("depth")),
        check_vma=False,
    )
```

```python
import functools

import jax
import jax.numpy as jnp
from jax import lax
from jax.experimental import pallas as pl
from jax.experimental.pallas import tpu as pltpu
from jax.sharding import PartitionSpec as P

F32 = jnp.float32
BF16 = jnp.bfloat16
VMEM = pl.BlockSpec(memory_space=pltpu.VMEM)
HBM = pl.BlockSpec(memory_space=pltpu.HBM)


def split_three(x):
    parts = []
    for _ in range(3):
        head = lax.reduce_precision(x, 8, 7)
        parts.append(head.astype(BF16))
        x = x - head
    return jnp.stack(parts)


def gather_blocks(block, axis):
    copies = jnp.broadcast_to(block[None], (lax.axis_size(axis),) + block.shape)
    return lax.all_to_all(copies, axis, 0, 0)


def dressing_kernel(bounds, vertex_ref, amplitudes_ref, out_ref, held_ref, sems):
    copies = []
    for at, (low, high) in enumerate(bounds):
        span = pl.ds(low, high - low)
        copy = pltpu.make_async_copy(amplitudes_ref.at[:, span], held_ref.at[:, span], sems.at[at])
        copy.start()
        copies.append(copy)
    vertex = vertex_ref[...].T
    for copy, (low, high) in zip(copies, bounds):
        copy.wait()
        part = jnp.dot(vertex, held_ref[:, low:high], preferred_element_type=F32)
        out_ref[low:high, :] = part.T.astype(BF16)


def dressing_part(vertex, amplitudes):
    pairs, fields = vertex.shape
    width = amplitudes.shape[1]
    edges = [0, 256, 512, 1024, 1536, 2048, width]
    bounds = list(zip(edges[:-1], edges[1:]))
    return pl.pallas_call(
        functools.partial(dressing_kernel, bounds),
        in_specs=[VMEM, HBM],
        out_specs=VMEM,
        out_shape=jax.ShapeDtypeStruct((width, fields), BF16),
        scratch_shapes=[
            pltpu.VMEM((pairs, width), BF16),
            pltpu.SemaphoreType.DMA((len(bounds),)),
        ],
        cost_estimate=pl.CostEstimate(
            flops=2 * pairs * fields * width, transcendentals=0, bytes_accessed=2 * pairs * width
        ),
        compiler_params=pltpu.CompilerParams(vmem_limit_bytes=52 << 20),
    )(vertex, amplitudes)


def residual_kernel(row_mine, row_other, col_mine, col_other, out_ref, turned):
    @pl.when(pl.program_id(0) == 0)
    def _():
        turned[:128, :] = col_mine[...].T
        turned[128:, :] = col_other[...].T

    left = jnp.concatenate([row_mine[...], row_other[...]], axis=1)
    out_ref[...] = jnp.dot(left, turned[...], preferred_element_type=F32).astype(BF16)


def residual(row_mine, row_other, col_mine, col_other):
    pairs, fields = row_mine.shape
    width = col_mine.shape[0]
    tile = 640
    tall = pl.BlockSpec((tile, fields), lambda i: (i, 0))
    whole = pl.BlockSpec((width, fields), lambda i: (0, 0))
    return pl.pallas_call(
        residual_kernel,
        grid=(pairs // tile,),
        in_specs=[tall, tall, whole, whole],
        out_specs=pl.BlockSpec((tile, width), lambda i: (i, 0)),
        out_shape=jax.ShapeDtypeStruct((pairs, width), BF16),
        scratch_shapes=[pltpu.VMEM((2 * fields, width), BF16)],
        cost_estimate=pl.CostEstimate(
            flops=4 * pairs * fields * width, transcendentals=0, bytes_accessed=2 * pairs * width
        ),
        compiler_params=pltpu.CompilerParams(vmem_limit_bytes=40 << 20),
    )(row_mine, row_other, col_mine, col_other)


def body(amplitudes, coulomb_vertex):
    rows = lax.axis_size("row")
    cols = lax.axis_size("col")
    fields, width = coulomb_vertex.shape
    row_index = lax.axis_index("row")
    col_index = lax.axis_index("col")
    depth_index = lax.axis_index("depth")

    shard, row_index, col_index = lax.optimization_barrier((coulomb_vertex.T, row_index, col_index))
    vertex_rows = gather_blocks(shard, "col").reshape(-1, fields)
    vertex_rows, row_index, col_index = lax.optimization_barrier((vertex_rows, row_index, col_index))

    def served(c, j):
        return 2 * (((c & ~1) + 2 - (j >> 1)) & 3) + (j & 1)

    pairs = [
        (c * cols + j, served(c, j) * cols + c) for c in range(rows) for j in range(cols)
    ]
    piece = lax.dynamic_slice_in_dim(vertex_rows, served(row_index, col_index) * width, width, 0)
    vertex_here = lax.ppermute(piece, ("row", "col"), pairs)
    partial = dressing_part(vertex_rows, amplitudes).reshape(rows, width, fields)
    partial, vertex_here = lax.optimization_barrier((partial, vertex_here))
    partial = lax.all_to_all(partial, "row", 0, 0)
    dressing = jnp.sum(partial.astype(F32), axis=0)
    vertex_here = vertex_here.astype(F32)
    factor = jnp.sum(vertex_here * dressing, axis=0)
    dressed = (vertex_here + dressing).astype(BF16)

    pad = jnp.zeros((13, fields), BF16)
    block = jnp.concatenate([dressed, split_three(factor), pad])
    along = gather_blocks(block, "col")
    factor = jnp.sum(along[:, width : width + 3].astype(F32), axis=(0, 1))
    tail = jnp.concatenate([dressed, split_three(factor), pad])
    chunks = jnp.concatenate(
        [along[:, :width], jnp.broadcast_to(tail[None], (rows,) + tail.shape)], axis=1
    )
    arrived = lax.all_to_all(chunks, "row", 0, 0)
    structure_factor = jnp.sum(arrived[:, 2 * width : 2 * width + 3].astype(F32), axis=(0, 1))
    row_block = arrived[:, :width].reshape(-1, fields)
    col_block = arrived[:, width : 2 * width].reshape(-1, fields)

    half = col_block.shape[0] // 2
    swap = [(0, 1), (1, 0)]
    cols_mine = lax.dynamic_slice_in_dim(col_block, depth_index * half, half, 0)
    cols_send = lax.dynamic_slice_in_dim(col_block, (1 - depth_index) * half, half, 0)
    cols_other = lax.ppermute(cols_send, "depth", swap)
    rows_other = lax.ppermute(row_block, "depth", swap)
    cycle_residual = residual(row_block, rows_other, cols_mine, cols_other)
    return (cycle_residual, structure_factor)


def solution(mesh):
    return jax.shard_map(
        body,
        mesh=mesh,
        in_specs=(P("row", "col"), P("depth", ("row", "col"))),
        out_specs=(P("row", ("col", "depth")), P("depth")),
        check_vma=False,
    )
```

```python
import functools

import jax
import jax.numpy as jnp
from jax import lax
from jax.experimental import pallas as pl
from jax.experimental.pallas import tpu as pltpu
from jax.sharding import PartitionSpec as P

F32 = jnp.float32
BF16 = jnp.bfloat16
VMEM = pl.BlockSpec(memory_space=pltpu.VMEM)
HBM = pl.BlockSpec(memory_space=pltpu.HBM)


def split_three(x):
    parts = []
    for _ in range(3):
        head = lax.reduce_precision(x, 8, 7)
        parts.append(head.astype(BF16))
        x = x - head
    return jnp.stack(parts)


def served_pair(c, pair):
    return ((c & ~1) + 2 - pair) & 3


def gather_blocks(block, axis):
    copies = jnp.broadcast_to(block[None], (lax.axis_size(axis),) + block.shape)
    return lax.all_to_all(copies, axis, 0, 0)


def dressing_kernel(bounds, vertex_ref, amplitudes_ref, out_ref, held_ref, sems):
    copies = []
    for at, (low, high) in enumerate(bounds):
        span = pl.ds(low, high - low)
        copy = pltpu.make_async_copy(amplitudes_ref.at[:, span], held_ref.at[:, span], sems.at[at])
        copy.start()
        copies.append(copy)
    vertex = vertex_ref[...].T
    for copy, (low, high) in zip(copies, bounds):
        copy.wait()
        part = jnp.dot(vertex, held_ref[:, low:high], preferred_element_type=F32)
        out_ref[low:high, :] = part.T.astype(BF16)


def dressing_part(vertex, amplitudes):
    pairs, fields = vertex.shape
    width = amplitudes.shape[1]
    edges = [0, 256, 512, 1024, 1536, 2048, width]
    bounds = list(zip(edges[:-1], edges[1:]))
    return pl.pallas_call(
        functools.partial(dressing_kernel, bounds),
        in_specs=[VMEM, HBM],
        out_specs=VMEM,
        out_shape=jax.ShapeDtypeStruct((width, fields), BF16),
        scratch_shapes=[
            pltpu.VMEM((pairs, width), BF16),
            pltpu.SemaphoreType.DMA((len(bounds),)),
        ],
        cost_estimate=pl.CostEstimate(
            flops=2 * pairs * fields * width, transcendentals=0, bytes_accessed=2 * pairs * width
        ),
        compiler_params=pltpu.CompilerParams(vmem_limit_bytes=52 << 20),
    )(vertex, amplitudes)


def residual_kernel(place_ref, row_mine, row_other, col_mine, col_other, out_ref, turned):
    @pl.when(pl.program_id(0) == 0)
    def _():
        turned[:128, :] = col_mine[...].T
        turned[128:, :] = col_other[...].T

    left = jnp.concatenate([row_mine[...], row_other[...]], axis=1)
    out_ref[...] = jnp.dot(left, turned[...], preferred_element_type=F32).astype(BF16)


def residual(place, row_mine, row_other, col_mine, col_other):
    pairs, fields = row_mine.shape
    width = col_mine.shape[0]
    tile = 640
    tiles = pairs // tile
    tall = pl.BlockSpec((tile, fields), lambda i, place: (i, 0))
    whole = pl.BlockSpec((width, fields), lambda i, place: (0, 0))
    return pl.pallas_call(
        residual_kernel,
        grid_spec=pltpu.PrefetchScalarGridSpec(
            num_scalar_prefetch=1,
            grid=(tiles,),
            in_specs=[tall, tall, whole, whole],
            out_specs=pl.BlockSpec((tile, width), lambda i, place: (served_pair(place[0], i), 0)),
            scratch_shapes=[pltpu.VMEM((2 * fields, width), BF16)],
        ),
        out_shape=jax.ShapeDtypeStruct((pairs, width), BF16),
        cost_estimate=pl.CostEstimate(
            flops=4 * pairs * fields * width, transcendentals=0, bytes_accessed=2 * pairs * width
        ),
        compiler_params=pltpu.CompilerParams(vmem_limit_bytes=40 << 20),
    )(place, row_mine, row_other, col_mine, col_other)


def settle_kernel(block_ref, out_ref):
    out_ref[...] = block_ref[...]


def settle(block, flops):
    return pl.pallas_call(
        settle_kernel,
        in_specs=[VMEM],
        out_specs=VMEM,
        out_shape=jax.ShapeDtypeStruct(block.shape, block.dtype),
        cost_estimate=pl.CostEstimate(flops=flops, transcendentals=0, bytes_accessed=4 * block.size),
        compiler_params=pltpu.CompilerParams(vmem_limit_bytes=4 << 20),
    )(block)


def body(amplitudes, coulomb_vertex):
    rows = lax.axis_size("row")
    cols = lax.axis_size("col")
    fields, width = coulomb_vertex.shape
    row_index = lax.axis_index("row")
    col_index = lax.axis_index("col")
    depth_index = lax.axis_index("depth")

    shard, row_index, col_index = lax.optimization_barrier((coulomb_vertex.T, row_index, col_index))
    vertex_rows = gather_blocks(shard, "col").reshape(-1, fields)
    vertex_rows, row_index, col_index = lax.optimization_barrier((vertex_rows, row_index, col_index))

    def served(c, j):
        return 2 * served_pair(c, j >> 1) + (j & 1)

    pairs = [
        (c * cols + j, served(c, j) * cols + c) for c in range(rows) for j in range(cols)
    ]
    piece = lax.dynamic_slice_in_dim(vertex_rows, served(row_index, col_index) * width, width, 0)
    vertex_here = lax.ppermute(piece, ("row", "col"), pairs)
    partial = dressing_part(vertex_rows, amplitudes).reshape(rows, width, fields)
    partial, vertex_here = lax.optimization_barrier((partial, vertex_here))
    partial = lax.all_to_all(partial, "row", 0, 0)
    dressing = jnp.sum(partial.astype(F32), axis=0)
    vertex_here = vertex_here.astype(F32)
    factor = jnp.sum(vertex_here * dressing, axis=0)
    dressed = (vertex_here + dressing).astype(BF16)

    moved = lax.ppermute(dressed, ("row", "col"), [(there, here) for here, there in pairs])
    moved = settle(moved, 30_000_000_000)
    pad = jnp.zeros((13, fields), BF16)
    block = jnp.concatenate([dressed, split_three(factor), pad])
    along = gather_blocks(block, "row")
    factor = jnp.sum(along[:, width : width + 3].astype(F32), axis=(0, 1))
    col_block = along[:, :width].reshape(-1, fields)
    half = col_block.shape[0] // 2
    swap = [(0, 1), (1, 0)]
    cols_mine = lax.dynamic_slice_in_dim(col_block, depth_index * half, half, 0)
    cols_send = lax.dynamic_slice_in_dim(col_block, (1 - depth_index) * half, half, 0)
    cols_other = lax.ppermute(cols_send, "depth", swap)

    block = jnp.concatenate([moved, split_three(factor), pad])
    along = gather_blocks(block, "col")
    structure_factor = jnp.sum(along[:, width : width + 3].astype(F32), axis=(0, 1))
    row_block = along[:, :width].reshape(-1, fields)
    rows_other = lax.ppermute(row_block, "depth", swap)
    place = row_index.reshape(1)
    cycle_residual = residual(place, row_block, rows_other, cols_mine, cols_other)
    return (cycle_residual, structure_factor)


def solution(mesh):
    return jax.shard_map(
        body,
        mesh=mesh,
        in_specs=(P("row", "col"), P("depth", ("row", "col"))),
        out_specs=(P("row", ("col", "depth")), P("depth")),
        check_vma=False,
    )
```

```python
import functools

import jax
import jax.numpy as jnp
from jax import lax
from jax.experimental import pallas as pl
from jax.experimental.pallas import tpu as pltpu
from jax.sharding import PartitionSpec as P

F32 = jnp.float32
BF16 = jnp.bfloat16
VMEM = pl.BlockSpec(memory_space=pltpu.VMEM)
SMEM = pl.BlockSpec(memory_space=pltpu.SMEM)
HBM = pl.BlockSpec(memory_space=pltpu.HBM)


def split_three(x):
    parts = []
    for _ in range(3):
        head = lax.reduce_precision(x, 8, 7)
        parts.append(head.astype(BF16))
        x = x - head
    return jnp.stack(parts)


def served_pair(c, pair):
    return ((c & ~1) + 2 - pair) & 3


def gather_blocks(block, axis):
    copies = jnp.broadcast_to(block[None], (lax.axis_size(axis),) + block.shape)
    return lax.all_to_all(copies, axis, 0, 0)


def dressing_kernel(bounds, vertex_ref, amplitudes_ref, out_ref, held_ref, sems):
    copies = []
    for at, (low, high) in enumerate(bounds):
        span = pl.ds(low, high - low)
        copy = pltpu.make_async_copy(amplitudes_ref.at[:, span], held_ref.at[:, span], sems.at[at])
        copy.start()
        copies.append(copy)
    vertex = vertex_ref[...].T
    for copy, (low, high) in zip(copies, bounds):
        copy.wait()
        part = jnp.dot(vertex, held_ref[:, low:high], preferred_element_type=F32)
        out_ref[low:high, :] = part.T.astype(BF16)


def dressing_part(vertex, amplitudes):
    pairs, fields = vertex.shape
    width = amplitudes.shape[1]
    edges = [0, 256, 512, 1024, 1536, 2048, width]
    bounds = list(zip(edges[:-1], edges[1:]))
    return pl.pallas_call(
        functools.partial(dressing_kernel, bounds),
        in_specs=[VMEM, HBM],
        out_specs=VMEM,
        out_shape=jax.ShapeDtypeStruct((width, fields), BF16),
        scratch_shapes=[
            pltpu.VMEM((pairs, width), BF16),
            pltpu.SemaphoreType.DMA((len(bounds),)),
        ],
        cost_estimate=pl.CostEstimate(
            flops=2 * pairs * fields * width, transcendentals=0, bytes_accessed=2 * pairs * width
        ),
        compiler_params=pltpu.CompilerParams(vmem_limit_bytes=52 << 20),
    )(vertex, amplitudes)


def residual_kernel(place_ref, row_mine, row_other, col_mine, col_other, out_ref, turned, stage, sems):
    fields = row_mine.shape[1]
    tiles, tile, _ = stage.shape
    turned[:fields, :] = col_mine[...].T
    turned[fields:, :] = col_other[...].T
    copies = []
    for at in range(tiles):
        span = slice(at * tile, (at + 1) * tile)
        left = jnp.concatenate([row_mine[span, :], row_other[span, :]], axis=1)
        stage[at] = jnp.dot(left, turned[...], preferred_element_type=F32).astype(BF16)
        to = pl.multiple_of(served_pair(place_ref[0], at) * tile, 128)
        copy = pltpu.make_async_copy(stage.at[at], out_ref.at[pl.ds(to, tile), :], sems.at[at])
        copy.start()
        copies.append(copy)
    for copy in copies:
        copy.wait()


def residual(place, row_mine, row_other, col_mine, col_other):
    pairs, fields = row_mine.shape
    width = col_mine.shape[0]
    tiles = 4
    return pl.pallas_call(
        residual_kernel,
        in_specs=[SMEM, VMEM, VMEM, VMEM, VMEM],
        out_specs=HBM,
        out_shape=jax.ShapeDtypeStruct((pairs, width), BF16),
        scratch_shapes=[
            pltpu.VMEM((2 * fields, width), BF16),
            pltpu.VMEM((tiles, pairs // tiles, width), BF16),
            pltpu.SemaphoreType.DMA((tiles,)),
        ],
        cost_estimate=pl.CostEstimate(
            flops=4 * pairs * fields * width, transcendentals=0, bytes_accessed=2 * pairs * width
        ),
        compiler_params=pltpu.CompilerParams(vmem_limit_bytes=40 << 20),
    )(place, row_mine, row_other, col_mine, col_other)


def settle_kernel(block_ref, out_ref):
    out_ref[...] = block_ref[...]


def settle(block, flops):
    return pl.pallas_call(
        settle_kernel,
        in_specs=[VMEM],
        out_specs=VMEM,
        out_shape=jax.ShapeDtypeStruct(block.shape, block.dtype),
        cost_estimate=pl.CostEstimate(flops=flops, transcendentals=0, bytes_accessed=4 * block.size),
        compiler_params=pltpu.CompilerParams(vmem_limit_bytes=4 << 20),
    )(block)


def body(amplitudes, coulomb_vertex):
    rows = lax.axis_size("row")
    cols = lax.axis_size("col")
    fields, width = coulomb_vertex.shape
    row_index = lax.axis_index("row")
    col_index = lax.axis_index("col")
    depth_index = lax.axis_index("depth")

    shard, row_index, col_index = lax.optimization_barrier((coulomb_vertex.T, row_index, col_index))
    vertex_rows = gather_blocks(shard, "col").reshape(-1, fields)
    vertex_rows, row_index, col_index = lax.optimization_barrier((vertex_rows, row_index, col_index))

    def served(c, j):
        return 2 * served_pair(c, j >> 1) + (j & 1)

    pairs = [
        (c * cols + j, served(c, j) * cols + c) for c in range(rows) for j in range(cols)
    ]
    piece = lax.dynamic_slice_in_dim(vertex_rows, served(row_index, col_index) * width, width, 0)
    vertex_here = lax.ppermute(piece, ("row", "col"), pairs)
    partial = dressing_part(vertex_rows, amplitudes).reshape(rows, width, fields)
    partial, vertex_here = lax.optimization_barrier((partial, vertex_here))
    partial = lax.all_to_all(partial, "row", 0, 0)
    dressing = jnp.sum(partial.astype(F32), axis=0)
    vertex_here = vertex_here.astype(F32)
    factor = jnp.sum(vertex_here * dressing, axis=0)
    dressed = (vertex_here + dressing).astype(BF16)

    moved = lax.ppermute(dressed, ("row", "col"), [(there, here) for here, there in pairs])
    moved = settle(moved, 30_000_000_000)
    pad = jnp.zeros((13, fields), BF16)
    block = jnp.concatenate([dressed, split_three(factor), pad])
    along = gather_blocks(block, "row")
    factor = jnp.sum(along[:, width : width + 3].astype(F32), axis=(0, 1))
    col_block = along[:, :width].reshape(-1, fields)
    half = col_block.shape[0] // 2
    swap = [(0, 1), (1, 0)]
    cols_mine = lax.dynamic_slice_in_dim(col_block, depth_index * half, half, 0)
    cols_send = lax.dynamic_slice_in_dim(col_block, (1 - depth_index) * half, half, 0)
    cols_other = lax.ppermute(cols_send, "depth", swap)

    block = jnp.concatenate([moved, split_three(factor), pad])
    along = gather_blocks(block, "col")
    structure_factor = jnp.sum(along[:, width : width + 3].astype(F32), axis=(0, 1))
    row_block = along[:, :width].reshape(-1, fields)
    rows_other = lax.ppermute(row_block, "depth", swap)
    place = row_index.reshape(1)
    cycle_residual = residual(place, row_block, rows_other, cols_mine, cols_other)
    return (cycle_residual, structure_factor)


def solution(mesh):
    return jax.shard_map(
        body,
        mesh=mesh,
        in_specs=(P("row", "col"), P("depth", ("row", "col"))),
        out_specs=(P("row", ("col", "depth")), P("depth")),
        check_vma=False,
    )
```

```python
import functools

import jax
import jax.numpy as jnp
from jax import lax
from jax.experimental import pallas as pl
from jax.experimental.pallas import tpu as pltpu
from jax.sharding import PartitionSpec as P

F32 = jnp.float32
BF16 = jnp.bfloat16
VMEM = pl.BlockSpec(memory_space=pltpu.VMEM)
SMEM = pl.BlockSpec(memory_space=pltpu.SMEM)
HBM = pl.BlockSpec(memory_space=pltpu.HBM)


def split_three(x):
    parts = []
    for _ in range(3):
        head = lax.reduce_precision(x, 8, 7)
        parts.append(head.astype(BF16))
        x = x - head
    return jnp.stack(parts)


def served_pair(c, pair):
    return ((c & ~1) + 2 - pair) & 3


def gather_blocks(block, axis):
    copies = jnp.broadcast_to(block[None], (lax.axis_size(axis),) + block.shape)
    return lax.all_to_all(copies, axis, 0, 0)


def dressing_kernel(bounds, vertex_ref, amplitudes_ref, out_ref, held_ref, sems):
    copies = []
    for at, (low, high) in enumerate(bounds):
        span = pl.ds(low, high - low)
        copy = pltpu.make_async_copy(amplitudes_ref.at[:, span], held_ref.at[:, span], sems.at[at])
        copy.start()
        copies.append(copy)
    vertex = vertex_ref[...].T
    for copy, (low, high) in zip(copies, bounds):
        copy.wait()
        part = jnp.dot(vertex, held_ref[:, low:high], preferred_element_type=F32)
        out_ref[low:high, :] = part.T.astype(BF16)


def dressing_part(vertex, amplitudes):
    pairs, fields = vertex.shape
    width = amplitudes.shape[1]
    edges = [0, 256, 512, 1024, 1536, 2048, width]
    bounds = list(zip(edges[:-1], edges[1:]))
    return pl.pallas_call(
        functools.partial(dressing_kernel, bounds),
        in_specs=[VMEM, HBM],
        out_specs=VMEM,
        out_shape=jax.ShapeDtypeStruct((width, fields), BF16),
        scratch_shapes=[
            pltpu.VMEM((pairs, width), BF16),
            pltpu.SemaphoreType.DMA((len(bounds),)),
        ],
        cost_estimate=pl.CostEstimate(
            flops=2 * pairs * fields * width, transcendentals=0, bytes_accessed=2 * pairs * width
        ),
        compiler_params=pltpu.CompilerParams(vmem_limit_bytes=52 << 20),
    )(vertex, amplitudes)


def residual_kernel(place_ref, row_mine, row_other, col_mine, col_other, out_ref, turned, stage, sems):
    fields = row_mine.shape[1]
    tiles, tile, _ = stage.shape
    turned[:fields, :] = col_mine[...].T
    turned[fields:, :] = col_other[...].T
    copies = []
    for at in range(tiles):
        span = slice(at * tile, (at + 1) * tile)
        left = jnp.concatenate([row_mine[span, :], row_other[span, :]], axis=1)
        stage[at] = jnp.dot(left, turned[...], preferred_element_type=F32).astype(BF16)
        to = pl.multiple_of(served_pair(place_ref[0], at) * tile, 128)
        copy = pltpu.make_async_copy(stage.at[at], out_ref.at[pl.ds(to, tile), :], sems.at[at])
        copy.start()
        copies.append(copy)
    for copy in copies:
        copy.wait()


def residual(place, row_mine, row_other, col_mine, col_other):
    pairs, fields = row_mine.shape
    width = col_mine.shape[0]
    tiles = 4
    return pl.pallas_call(
        residual_kernel,
        in_specs=[SMEM, VMEM, VMEM, VMEM, VMEM],
        out_specs=HBM,
        out_shape=jax.ShapeDtypeStruct((pairs, width), BF16),
        scratch_shapes=[
            pltpu.VMEM((2 * fields, width), BF16),
            pltpu.VMEM((tiles, pairs // tiles, width), BF16),
            pltpu.SemaphoreType.DMA((tiles,)),
        ],
        cost_estimate=pl.CostEstimate(
            flops=4 * pairs * fields * width, transcendentals=0, bytes_accessed=2 * pairs * width
        ),
        compiler_params=pltpu.CompilerParams(vmem_limit_bytes=40 << 20),
    )(place, row_mine, row_other, col_mine, col_other)


def settle_kernel(block_ref, out_ref):
    out_ref[...] = block_ref[...]


def settle(block, flops):
    return pl.pallas_call(
        settle_kernel,
        in_specs=[VMEM],
        out_specs=VMEM,
        out_shape=jax.ShapeDtypeStruct(block.shape, block.dtype),
        cost_estimate=pl.CostEstimate(flops=flops, transcendentals=0, bytes_accessed=4 * block.size),
        compiler_params=pltpu.CompilerParams(vmem_limit_bytes=4 << 20),
    )(block)


def body(amplitudes, coulomb_vertex):
    rows = lax.axis_size("row")
    cols = lax.axis_size("col")
    fields, width = coulomb_vertex.shape
    row_index = lax.axis_index("row")
    col_index = lax.axis_index("col")
    depth_index = lax.axis_index("depth")

    shard, row_index, col_index = lax.optimization_barrier((coulomb_vertex.T, row_index, col_index))
    vertex_rows = gather_blocks(shard, "col").reshape(-1, fields)
    vertex_rows, row_index, col_index = lax.optimization_barrier((vertex_rows, row_index, col_index))

    def served(c, j):
        return 2 * served_pair(c, j >> 1) + (j & 1)

    pairs = [
        (c * cols + j, served(c, j) * cols + c) for c in range(rows) for j in range(cols)
    ]
    piece = lax.dynamic_slice_in_dim(vertex_rows, served(row_index, col_index) * width, width, 0)
    vertex_here = lax.ppermute(piece, ("row", "col"), pairs)
    partial = dressing_part(vertex_rows, amplitudes).reshape(rows, width, fields)
    partial, vertex_here = lax.optimization_barrier((partial, vertex_here))
    partial = lax.all_to_all(partial, "row", 0, 0)
    dressing = jnp.sum(partial.astype(F32), axis=0)
    vertex_here = vertex_here.astype(F32)
    factor = jnp.sum(vertex_here * dressing, axis=0)
    dressed = (vertex_here + dressing).astype(BF16)

    moved = lax.ppermute(dressed, ("row", "col"), [(there, here) for here, there in pairs])
    moved = settle(moved, 30_000_000_000)
    pad = jnp.zeros((5, fields), BF16)
    block = jnp.concatenate([dressed, split_three(factor), pad])
    along = gather_blocks(block, "row")
    factor = jnp.sum(along[:, width : width + 3].astype(F32), axis=(0, 1))
    col_block = along[:, :width].reshape(-1, fields)
    half = col_block.shape[0] // 2
    swap = [(0, 1), (1, 0)]
    cols_mine = lax.dynamic_slice_in_dim(col_block, depth_index * half, half, 0)
    cols_send = lax.dynamic_slice_in_dim(col_block, (1 - depth_index) * half, half, 0)
    cols_other = lax.ppermute(cols_send, "depth", swap)

    block = jnp.concatenate([moved, split_three(factor), pad])
    along = gather_blocks(block, "col")
    structure_factor = jnp.sum(along[:, width : width + 3].astype(F32), axis=(0, 1))
    row_block = along[:, :width].reshape(-1, fields)
    rows_other = lax.ppermute(row_block, "depth", swap)
    place = row_index.reshape(1)
    cycle_residual = residual(place, row_block, rows_other, cols_mine, cols_other)
    return (cycle_residual, structure_factor)


def solution(mesh):
    return jax.shard_map(
        body,
        mesh=mesh,
        in_specs=(P("row", "col"), P("depth", ("row", "col"))),
        out_specs=(P("row", ("col", "depth")), P("depth")),
        check_vma=False,
    )
```

```python
import functools

import jax
import jax.numpy as jnp
from jax import lax
from jax.experimental import pallas as pl
from jax.experimental.pallas import tpu as pltpu
from jax.sharding import PartitionSpec as P

F32 = jnp.float32
BF16 = jnp.bfloat16
VMEM = pl.BlockSpec(memory_space=pltpu.VMEM)
SMEM = pl.BlockSpec(memory_space=pltpu.SMEM)
HBM = pl.BlockSpec(memory_space=pltpu.HBM)


def split_three(x):
    parts = []
    for _ in range(3):
        head = lax.reduce_precision(x, 8, 7)
        parts.append(head.astype(BF16))
        x = x - head
    return jnp.stack(parts)


def served_pair(c, pair):
    return ((c & ~1) + 2 - pair) & 3


def gather_blocks(block, axis):
    copies = jnp.broadcast_to(block[None], (lax.axis_size(axis),) + block.shape)
    return lax.all_to_all(copies, axis, 0, 0)


def dressing_kernel(bounds, vertex_ref, amplitudes_ref, out_ref, held_ref, sems):
    copies = []
    for at, (low, high) in enumerate(bounds):
        span = pl.ds(low, high - low)
        copy = pltpu.make_async_copy(amplitudes_ref.at[:, span], held_ref.at[:, span], sems.at[at])
        copy.start()
        copies.append(copy)
    vertex = vertex_ref[...].T
    for copy, (low, high) in zip(copies, bounds):
        copy.wait()
        part = jnp.dot(vertex, held_ref[:, low:high], preferred_element_type=F32)
        out_ref[low:high, :] = part.T.astype(BF16)


def dressing_part(vertex, amplitudes):
    pairs, fields = vertex.shape
    width = amplitudes.shape[1]
    edges = [0, 256, 512, 1024, 1536, 2048, width]
    bounds = list(zip(edges[:-1], edges[1:]))
    return pl.pallas_call(
        functools.partial(dressing_kernel, bounds),
        in_specs=[VMEM, HBM],
        out_specs=VMEM,
        out_shape=jax.ShapeDtypeStruct((width, fields), BF16),
        scratch_shapes=[
            pltpu.VMEM((pairs, width), BF16),
            pltpu.SemaphoreType.DMA((len(bounds),)),
        ],
        cost_estimate=pl.CostEstimate(
            flops=2 * pairs * fields * width, transcendentals=0, bytes_accessed=2 * pairs * width
        ),
        compiler_params=pltpu.CompilerParams(vmem_limit_bytes=52 << 20),
    )(vertex, amplitudes)


def residual_kernel(place_ref, row_mine, row_other, col_mine, col_other, out_ref, turned, stage, sems):
    fields = row_mine.shape[1]
    tiles, tile, _ = stage.shape
    turned[:fields, :] = col_mine[...]
    turned[fields:, :] = col_other[...].T
    copies = []
    for at in range(tiles):
        span = slice(at * tile, (at + 1) * tile)
        left = jnp.concatenate([row_mine[span, :], row_other[span, :]], axis=1)
        stage[at] = jnp.dot(left, turned[...], preferred_element_type=F32).astype(BF16)
        to = pl.multiple_of(served_pair(place_ref[0], at) * tile, 128)
        copy = pltpu.make_async_copy(stage.at[at], out_ref.at[pl.ds(to, tile), :], sems.at[at])
        copy.start()
        copies.append(copy)
    for copy in copies:
        copy.wait()


def residual(place, row_mine, row_other, col_mine, col_other):
    pairs, fields = row_mine.shape
    width = col_mine.shape[1]
    tiles = 4
    return pl.pallas_call(
        residual_kernel,
        in_specs=[SMEM, VMEM, VMEM, VMEM, VMEM],
        out_specs=HBM,
        out_shape=jax.ShapeDtypeStruct((pairs, width), BF16),
        scratch_shapes=[
            pltpu.VMEM((2 * fields, width), BF16),
            pltpu.VMEM((tiles, pairs // tiles, width), BF16),
            pltpu.SemaphoreType.DMA((tiles,)),
        ],
        cost_estimate=pl.CostEstimate(
            flops=4 * pairs * fields * width, transcendentals=0, bytes_accessed=2 * pairs * width
        ),
        compiler_params=pltpu.CompilerParams(vmem_limit_bytes=40 << 20),
    )(place, row_mine, row_other, col_mine, col_other)


def settle_kernel(block_ref, out_ref):
    out_ref[...] = block_ref[...]


def settle(block, flops):
    return pl.pallas_call(
        settle_kernel,
        in_specs=[VMEM],
        out_specs=VMEM,
        out_shape=jax.ShapeDtypeStruct(block.shape, block.dtype),
        cost_estimate=pl.CostEstimate(flops=flops, transcendentals=0, bytes_accessed=4 * block.size),
        compiler_params=pltpu.CompilerParams(vmem_limit_bytes=4 << 20),
    )(block)


def body(amplitudes, coulomb_vertex):
    rows = lax.axis_size("row")
    cols = lax.axis_size("col")
    fields, width = coulomb_vertex.shape
    row_index = lax.axis_index("row")
    col_index = lax.axis_index("col")
    depth_index = lax.axis_index("depth")

    shard, row_index, col_index = lax.optimization_barrier((coulomb_vertex.T, row_index, col_index))
    vertex_rows = gather_blocks(shard, "col").reshape(-1, fields)
    vertex_rows, row_index, col_index = lax.optimization_barrier((vertex_rows, row_index, col_index))

    def served(c, j):
        return 2 * served_pair(c, j >> 1) + (j & 1)

    pairs = [
        (c * cols + j, served(c, j) * cols + c) for c in range(rows) for j in range(cols)
    ]
    piece = lax.dynamic_slice_in_dim(vertex_rows, served(row_index, col_index) * width, width, 0)
    vertex_here = lax.ppermute(piece, ("row", "col"), pairs)
    partial = dressing_part(vertex_rows, amplitudes).reshape(rows, width, fields)
    partial, vertex_here = lax.optimization_barrier((partial, vertex_here))
    partial = lax.all_to_all(partial, "row", 0, 0)
    dressing = jnp.sum(partial.astype(F32), axis=0)
    vertex_here = vertex_here.astype(F32)
    factor = jnp.sum(vertex_here * dressing, axis=0)
    dressed = (vertex_here + dressing).astype(BF16)

    moved = lax.ppermute(dressed, ("row", "col"), [(there, here) for here, there in pairs])
    moved = settle(moved, 30_000_000_000)
    pad = jnp.zeros((5, fields), BF16)
    block = jnp.concatenate([dressed, split_three(factor), pad])
    along = gather_blocks(block, "row")
    factor = jnp.sum(along[:, width : width + 3].astype(F32), axis=(0, 1))
    col_block = along[:, :width].reshape(-1, fields)
    half = col_block.shape[0] // 2
    swap = [(0, 1), (1, 0)]
    cols_mine = lax.dynamic_slice_in_dim(col_block, depth_index * half, half, 0)
    cols_send = lax.dynamic_slice_in_dim(col_block, (1 - depth_index) * half, half, 0)
    cols_other = lax.ppermute(cols_send, "depth", swap)

    block = jnp.concatenate([moved, split_three(factor), pad])
    along = gather_blocks(block, "col")
    structure_factor = jnp.sum(along[:, width : width + 3].astype(F32), axis=(0, 1))
    row_block = along[:, :width].reshape(-1, fields)
    rows_other = lax.ppermute(row_block, "depth", swap)
    place = row_index.reshape(1)
    cycle_residual = residual(place, row_block, rows_other, cols_mine.T, cols_other)
    return (cycle_residual, structure_factor)


def solution(mesh):
    return jax.shard_map(
        body,
        mesh=mesh,
        in_specs=(P("row", "col"), P("depth", ("row", "col"))),
        out_specs=(P("row", ("col", "depth")), P("depth")),
        check_vma=False,
    )
```

```python
import functools

import jax
import jax.numpy as jnp
from jax import lax
from jax.experimental import pallas as pl
from jax.experimental.pallas import tpu as pltpu
from jax.sharding import PartitionSpec as P

F32 = jnp.float32
BF16 = jnp.bfloat16
VMEM = pl.BlockSpec(memory_space=pltpu.VMEM)
SMEM = pl.BlockSpec(memory_space=pltpu.SMEM)
HBM = pl.BlockSpec(memory_space=pltpu.HBM)


def split_three(x):
    parts = []
    for _ in range(3):
        head = lax.reduce_precision(x, 8, 7)
        parts.append(head.astype(BF16))
        x = x - head
    return jnp.stack(parts)


def served_pair(c, pair):
    return ((c >> 1) + 2 + (2 * (c & 1) - 1) * (pair - (c >> 1))) & 3


def gather_blocks(block, axis):
    copies = jnp.broadcast_to(block[None], (lax.axis_size(axis),) + block.shape)
    return lax.all_to_all(copies, axis, 0, 0)


def dressing_kernel(bounds, vertex_ref, amplitudes_ref, out_ref, held_ref, sems):
    copies = []
    for at, (low, high) in enumerate(bounds):
        span = pl.ds(low, high - low)
        copy = pltpu.make_async_copy(amplitudes_ref.at[:, span], held_ref.at[:, span], sems.at[at])
        copy.start()
        copies.append(copy)
    vertex = vertex_ref[...].T
    for copy, (low, high) in zip(copies, bounds):
        copy.wait()
        part = jnp.dot(vertex, held_ref[:, low:high], preferred_element_type=F32)
        out_ref[low:high, :] = part.T.astype(BF16)


def dressing_part(vertex, amplitudes):
    pairs, fields = vertex.shape
    width = amplitudes.shape[1]
    edges = [0, 256, 512, 1024, 1536, 2048, width]
    bounds = list(zip(edges[:-1], edges[1:]))
    return pl.pallas_call(
        functools.partial(dressing_kernel, bounds),
        in_specs=[VMEM, HBM],
        out_specs=VMEM,
        out_shape=jax.ShapeDtypeStruct((width, fields), BF16),
        scratch_shapes=[
            pltpu.VMEM((pairs, width), BF16),
            pltpu.SemaphoreType.DMA((len(bounds),)),
        ],
        cost_estimate=pl.CostEstimate(
            flops=2 * pairs * fields * width, transcendentals=0, bytes_accessed=2 * pairs * width
        ),
        compiler_params=pltpu.CompilerParams(vmem_limit_bytes=52 << 20),
    )(vertex, amplitudes)


def residual_kernel(place_ref, row_mine, row_other, col_mine, col_other, out_ref, turned, stage, sems):
    fields = row_mine.shape[1]
    tiles, tile, _ = stage.shape
    turned[:fields, :] = col_mine[...]
    turned[fields:, :] = col_other[...].T
    copies = []
    for at in range(tiles):
        span = slice(at * tile, (at + 1) * tile)
        left = jnp.concatenate([row_mine[span, :], row_other[span, :]], axis=1)
        stage[at] = jnp.dot(left, turned[...], preferred_element_type=F32).astype(BF16)
        to = pl.multiple_of(served_pair(place_ref[0], at) * tile, 128)
        copy = pltpu.make_async_copy(stage.at[at], out_ref.at[pl.ds(to, tile), :], sems.at[at])
        copy.start()
        copies.append(copy)
    for copy in copies:
        copy.wait()


def residual(place, row_mine, row_other, col_mine, col_other):
    pairs, fields = row_mine.shape
    width = col_mine.shape[1]
    tiles = 4
    return pl.pallas_call(
        residual_kernel,
        in_specs=[SMEM, VMEM, VMEM, VMEM, VMEM],
        out_specs=HBM,
        out_shape=jax.ShapeDtypeStruct((pairs, width), BF16),
        scratch_shapes=[
            pltpu.VMEM((2 * fields, width), BF16),
            pltpu.VMEM((tiles, pairs // tiles, width), BF16),
            pltpu.SemaphoreType.DMA((tiles,)),
        ],
        cost_estimate=pl.CostEstimate(
            flops=4 * pairs * fields * width, transcendentals=0, bytes_accessed=2 * pairs * width
        ),
        compiler_params=pltpu.CompilerParams(vmem_limit_bytes=40 << 20),
    )(place, row_mine, row_other, col_mine, col_other)


def settle_kernel(block_ref, out_ref):
    out_ref[...] = block_ref[...]


def settle(block, flops):
    return pl.pallas_call(
        settle_kernel,
        in_specs=[VMEM],
        out_specs=VMEM,
        out_shape=jax.ShapeDtypeStruct(block.shape, block.dtype),
        cost_estimate=pl.CostEstimate(flops=flops, transcendentals=0, bytes_accessed=4 * block.size),
        compiler_params=pltpu.CompilerParams(vmem_limit_bytes=4 << 20),
    )(block)


def body(amplitudes, coulomb_vertex):
    rows = lax.axis_size("row")
    cols = lax.axis_size("col")
    fields, width = coulomb_vertex.shape
    row_index = lax.axis_index("row")
    col_index = lax.axis_index("col")
    depth_index = lax.axis_index("depth")

    shard, row_index, col_index = lax.optimization_barrier((coulomb_vertex.T, row_index, col_index))
    vertex_rows = gather_blocks(shard, "col").reshape(-1, fields)
    vertex_rows, row_index, col_index = lax.optimization_barrier((vertex_rows, row_index, col_index))

    def served(c, j):
        return 2 * served_pair(c, j >> 1) + (j & 1)

    pairs = [
        (c * cols + j, served(c, j) * cols + c) for c in range(rows) for j in range(cols)
    ]
    piece = lax.dynamic_slice_in_dim(vertex_rows, served(row_index, col_index) * width, width, 0)
    vertex_here = lax.ppermute(piece, ("row", "col"), pairs)
    partial = dressing_part(vertex_rows, amplitudes).reshape(rows, width, fields)
    partial, vertex_here = lax.optimization_barrier((partial, vertex_here))
    partial = lax.all_to_all(partial, "row", 0, 0)
    dressing = jnp.sum(partial.astype(F32), axis=0)
    vertex_here = vertex_here.astype(F32)
    factor = jnp.sum(vertex_here * dressing, axis=0)
    dressed = (vertex_here + dressing).astype(BF16)

    moved = lax.ppermute(dressed, ("row", "col"), [(there, here) for here, there in pairs])
    moved = settle(moved, 30_000_000_000)
    pad = jnp.zeros((5, fields), BF16)
    block = jnp.concatenate([dressed, split_three(factor), pad])
    along = gather_blocks(block, "row")
    factor = jnp.sum(along[:, width : width + 3].astype(F32), axis=(0, 1))
    col_block = along[:, :width].reshape(-1, fields)
    half = col_block.shape[0] // 2
    swap = [(0, 1), (1, 0)]
    cols_mine = lax.dynamic_slice_in_dim(col_block, depth_index * half, half, 0)
    cols_send = lax.dynamic_slice_in_dim(col_block, (1 - depth_index) * half, half, 0)
    cols_other = lax.ppermute(cols_send, "depth", swap)

    block = jnp.concatenate([moved, split_three(factor), pad])
    along = gather_blocks(block, "col")
    structure_factor = jnp.sum(along[:, width : width + 3].astype(F32), axis=(0, 1))
    row_block = along[:, :width].reshape(-1, fields)
    rows_other = lax.ppermute(row_block, "depth", swap)
    place = row_index.reshape(1)
    cycle_residual = residual(place, row_block, rows_other, cols_mine.T, cols_other)
    return (cycle_residual, structure_factor)


def solution(mesh):
    return jax.shard_map(
        body,
        mesh=mesh,
        in_specs=(P("row", "col"), P("depth", ("row", "col"))),
        out_specs=(P("row", ("col", "depth")), P("depth")),
        check_vma=False,
    )
```
